768 devices in a mesh: energy: 16 (over y, core), kpt: 48 (over z, x).
Axes of the slice: x: 4, y: 8, z: 12, core: 2. Of those that a mesh axis runs over, the one named last changes fastest.
Arguments:
- onsite: float32 [48, 8, 64], P('kpt'), may hold values from -1 to 0
- hamil: float32 [48, 6, 2, 64, 64], P('kpt'), may hold values from -0.5 to 0.5
- coupling: float32 [48, 5, 2, 64, 64], P('kpt'), may hold values from -0.75 to 0.75
- lead_onsite: float32 [32, 48, 2, 2, 64, 64], P('energy', 'kpt'), may hold values from -0.1875 to 0.1875
- lead_hop: float32 [32, 48, 2, 2, 64, 64], P('energy', 'kpt'), may hold values from -0.5 to 2
- counts: int32 [32], replicated, may hold values from 1 to 4
- kernel: float32 [4, 48], replicated, may hold values from -2 to 2
- offsets: int32 [4], replicated, may hold values from 1 to 4
Outputs:
- sigma: float32 [32, 48, 6, 2, 64, 64], P('energy', 'kpt')
- lead_sigma: float32 [32, 48, 2, 2, 64, 64], P('energy', 'kpt')
The draws below stay inside these ranges and needn't reach their ends.
All inputs are finite; a program needn't handle non-finite values.
Results may differ from the reference program's by a relative error of at most 0.0003.
Values sent between devices are 32-bit elements; how exact they have to be, the bound alone decides.
A program may use at most 128 MiB of HBM per device.

```python
import jax
import jax.numpy as jnp
from jax import lax

NORB = 64
NB = 6
MAXIT = 4
NEWTON = 3
NMODE = 4
E_DEV = 2
NE = 32
K = 48


def draw_counts(key, part):
    base_key, spot_key, heavy_key = jax.random.split(jax.random.fold_in(key, 17), 3)
    baseline = jax.random.randint(base_key, (NE,), 1, 3)
    heavy = jax.random.randint(heavy_key, (NE,), MAXIT - 1, MAXIT + 1)
    opening = jax.random.randint(spot_key, (), 0, NE)
    place = (jnp.arange(NE, dtype=jnp.int32) - opening) % NE
    window = max(NE // 4, 2)
    result = jnp.where(place < window, heavy, baseline)
    result = jnp.where(place == 0, MAXIT, result)
    result = jnp.where(place == window, 1, result)
    return result.astype(jnp.int32)


def draw_lead_hop(key, part):
    diag_key, noise_key = jax.random.split(jax.random.fold_in(key, 29))
    energy_share = jnp.arange(NE, dtype=jnp.float32) / NE
    shape_full = (NE, K, 2, 2, NORB, NORB)
    factor = 0.8
    noise = jnp.clip(jax.random.normal(noise_key, shape_full, jnp.float32), -6.0, 6.0)
    strength = factor * (3.0 + energy_share) / 2.0
    strength = strength[:, None, None, None, None, None]
    orbital_gain = jax.random.uniform(diag_key, (NE, K, 2, 1, NORB, 1), jnp.float32, 0.95, 1.05)
    width = 0.2 / (2.0 * (NORB - 1)) ** 0.5
    identity = jnp.eye(NORB, dtype=jnp.float32)
    real_mask = jnp.array([1.0, 0.0], dtype=jnp.float32)[None, None, None, :, None, None]
    diagonal_part = identity[None, None, None, None, :, :] * real_mask * orbital_gain * strength
    return (noise * width * strength + diagonal_part).astype(jnp.float32)


def with_ends(drawn, key, least, largest):
    longest = drawn.shape.index(max(drawn.shape))
    spots = []
    for shift in (0, 1):
        where = [jax.random.randint(jax.random.fold_in(key, axis), (), 0, length) for axis, length in enumerate(drawn.shape)]
        where[longest] = (where[longest] + shift) % drawn.shape[longest]
        spots.append(tuple(where))
    return drawn.at[spots[0]].set(least).at[spots[1]].set(largest)


def steps_of(key, dims, cuts, smallest, top_value):
    def one(dim, parts):
        steps = jax.random.uniform(jax.random.fold_in(jax.random.fold_in(key, 6), dim), (parts,), jnp.float32, smallest / len(cuts), top_value / len(cuts))
        return jnp.repeat(jnp.exp(steps), dims[dim] // parts).reshape((-1,) + (1,) * (len(dims) - dim - 1))

    loudness = one(*cuts[0])
    for cut in cuts[1:]:
        loudness = loudness * one(*cut)
    return loudness


def centred(stream_key, extent, scale, most, shards=(), kind=jnp.bfloat16):
    values = scale * jax.random.normal(stream_key, extent, jnp.float32)
    if shards:
        values = values * steps_of(stream_key, extent, shards, -0.22, 0.18)
    return jnp.clip(values, -most, most).astype(kind)


def setup_inputs(seed: int = 0) -> dict:
    seeds = jax.random.split(jax.random.key(seed), 9)
    return {
        "onsite": jnp.clip(-1.0 + 1.0 * jax.random.uniform(seeds[0], (K, NB + 2, NORB), jnp.float32) ** steps_of(seeds[0], (K, NB + 2, NORB), ((0, 48),), -0.2, 0.2), -1.0, 0.0),
        "hamil": centred(seeds[1], (K, NB, 2, NORB, NORB), (0.25 / NORB ** 0.5), 0.5, ((0, 48),), jnp.float32),
        "coupling": centred(seeds[2], (K, NB - 1, 2, NORB, NORB), (0.4 / NORB ** 0.5), 0.75, ((0, 48),), jnp.float32),
        "lead_onsite": centred(seeds[3], (NE, K, 2, 2, NORB, NORB), (0.1 / NORB ** 0.5), 0.1875, ((0, 16), (1, 48)), jnp.float32),
        "lead_hop": draw_lead_hop(jax.random.fold_in(seeds[8], 71), 0),
        "counts": draw_counts(jax.random.fold_in(seeds[8], 71), 0),
        "kernel": centred(seeds[6], (NMODE, K), (3.0 / (2 * NMODE * K) ** 0.5), 2.0, (), jnp.float32),
        "offsets": with_ends(jax.random.randint(seeds[7], (NMODE,), 1, 2 * E_DEV + 1), jax.random.fold_in(seeds[7], 1), 1, 2 * E_DEV).astype(jnp.int32),
    }


BASE_ENERGY = 3.0
BROADENING = 0.1
HIGHEST = lax.Precision.HIGHEST


def product(left_side, right_side):
    return jnp.dot(left_side, right_side, precision=HIGHEST, preferred_element_type=jnp.float32)


def paired(block):
    upper_half = jnp.concatenate([block[0], -block[1]], axis=1)
    lower_half = jnp.concatenate([block[1], block[0]], axis=1)
    return jnp.concatenate([upper_half, lower_half], axis=0)


def compact(matrix):
    width = matrix.shape[0] // 2
    return jnp.stack([matrix[:width, :width], matrix[width:, :width]])


def diagonal_pair(real_part, imag_part):
    return paired(jnp.stack([jnp.diag(real_part), jnp.diag(imag_part)]))


def start_inverse(real_part, imag_part):
    modulus = real_part * real_part + imag_part * imag_part
    return diagonal_pair(real_part / modulus, -imag_part / modulus)


def newton_inverse(matrix, approx):
    doubled = 2.0 * jnp.eye(matrix.shape[0], dtype=jnp.float32)
    for number in range(NEWTON):
        approx = product(approx, doubled - product(matrix, approx))
    return approx


def lead_reference(real_part, imag_part, onsite_block, hop_block, repeats):
    start_guess = start_inverse(real_part, imag_part)
    bare_block = diagonal_pair(real_part, imag_part) - paired(onsite_block)
    hopping = paired(hop_block)

    def advance(number, surface):
        fresh = newton_inverse(bare_block - product(hopping.T, product(surface, hopping)), start_guess)
        return jnp.where(number < repeats, fresh, surface)

    surface = lax.fori_loop(0, MAXIT, advance, start_guess)
    return compact(product(hopping.T, product(surface, hopping)))


def sweep(real_part, imag_part, hamil_k, coupling_k, left_sigma, right_sigma):
    forward = []
    for segment in range(NB):
        matrix = diagonal_pair(real_part[segment], imag_part[segment]) - paired(hamil_k[segment])
        if segment == 0:
            matrix = matrix - paired(left_sigma)
        if segment == NB - 1:
            matrix = matrix - paired(right_sigma)
        if segment > 0:
            link = paired(coupling_k[segment - 1])
            matrix = matrix - product(link.T, product(forward[-1], link))
        forward.append(newton_inverse(matrix, start_inverse(real_part[segment], imag_part[segment])))
    greens = [forward[-1]]
    for segment in range(NB - 2, -1, -1):
        link = paired(coupling_k[segment])
        left_part = product(forward[segment], link)
        right_part = product(link.T, forward[segment])
        greens.insert(0, forward[segment] + product(left_part, product(greens[0], right_part)))
    return jnp.stack([compact(matrix) for matrix in greens])


def convolve(flattened, kernel, offsets):
    energy_count = flattened.shape[0]
    momenta = flattened.shape[1]
    momentum_axis = jnp.arange(momenta, dtype=jnp.int32)
    difference = (momentum_axis[:, None] - momentum_axis[None, :]) % momenta
    selector = (difference[None, :, :] == momentum_axis[:, None, None]).astype(jnp.float32)
    circulant = jnp.einsum('mq,qkj->mkj', kernel, selector, precision=HIGHEST)
    padded = jnp.pad(flattened, ((energy_count, energy_count), (0, 0), (0, 0)))
    result = jnp.zeros_like(flattened)
    for mode_number in range(NMODE):
        offset_now = offsets[mode_number]
        raised = lax.dynamic_slice_in_dim(padded, energy_count + offset_now, energy_count, 0)
        lowered = lax.dynamic_slice_in_dim(padded, energy_count - offset_now, energy_count, 0)
        result = result + jnp.einsum('kj,ejf->ekf', circulant[mode_number], raised + lowered, precision=HIGHEST)
    return result


def reference(onsite, hamil, coupling, lead_onsite, lead_hop, counts, kernel, offsets):
    energy_count = counts.shape[0]

    def one_energy(position):
        energy = BASE_ENERGY + position.astype(jnp.float32) / energy_count
        repeats = counts[position]

        def one_point(onsite_k, hamil_k, coupling_k, lead_on, lead_hp):
            real_part = energy - onsite_k
            imag_part = BROADENING * jnp.ones_like(onsite_k)
            left_sigma = lead_reference(real_part[NB], imag_part[NB], lead_on[0], lead_hp[0], repeats)
            right_sigma = lead_reference(real_part[NB + 1], imag_part[NB + 1], lead_on[1], lead_hp[1], repeats)
            greens = sweep(real_part[:NB], imag_part[:NB], hamil_k, coupling_k, left_sigma, right_sigma)
            return greens, jnp.stack([left_sigma, right_sigma])

        return jax.vmap(one_point)(onsite, hamil, coupling, lead_onsite[position], lead_hop[position])

    greens, lead_sigma = lax.map(one_energy, jnp.arange(energy_count, dtype=jnp.int32))
    flattened = greens.reshape(energy_count, greens.shape[1], -1)
    sigma = convolve(flattened, kernel, offsets).reshape(greens.shape)
    return sigma, lead_sigma
```

```python
import jax
import jax.numpy as jnp
from jax import lax
from jax.experimental import pallas as pl
from jax.experimental.pallas import tpu as pltpu
from jax.sharding import PartitionSpec as P

NORB = 64
W2 = 128
NB = 6
NMODE = 4
BASE_ENERGY = 3.0
BROADENING = 0.1
F32 = jnp.float32
BF16 = jnp.bfloat16
HIGHEST = lax.Precision.HIGHEST


def paired(real, imag):
    upper = jnp.concatenate([real, -imag], axis=1)
    lower = jnp.concatenate([imag, real], axis=1)
    return jnp.concatenate([upper, lower], axis=0)


def split(x):
    high = x.astype(BF16)
    low = (x - high.astype(F32)).astype(BF16)
    return jnp.concatenate([high, low], axis=1)


def tall(x):
    s = split(x)
    return jnp.concatenate([s, s], axis=0)


def mm(left, right):
    o = jnp.dot(left, right, preferred_element_type=F32)
    return o[:, :W2] + o[:, W2:]


def double(s):
    return jnp.concatenate([s, s], axis=0)


def swap_rows(x):
    return jnp.concatenate([x[NORB:], x[:NORB]], axis=0)


def times_diag(x, arow, brow):
    return x * arow + pltpu.roll(x, NORB, 1) * brow


def diag_times(x, acol, bcol):
    return x * acol + swap_rows(x) * bcol


def compute_kernel(counts_ref, onsite_ref, hamil_ref, coupling_ref, lon_ref, lhop_ref, green_ref, lead_ref,
                   l0_s, tf_s, ts_s, z0_s, sig_s):
    pos = lax.axis_index("energy")
    ids = [pos * 2, pos * 2 + 1]
    reps = [counts_ref[i] for i in ids]
    onsite = onsite_ref[...]
    onsite2 = jnp.concatenate([onsite, onsite], axis=1)
    lane = lax.broadcasted_iota(jnp.int32, (8, W2), 1)
    sign = jnp.where(lane < NORB, 1.0, -1.0).astype(F32)
    arow, brow, acol, bcol = [], [], [], []
    for e in range(2):
        energy = BASE_ENERGY + ids[e].astype(F32) * (1.0 / 32.0)
        re = energy - onsite2
        mod = re * re + BROADENING * BROADENING
        a = re / mod
        b = (-BROADENING / mod) * sign
        arow.append(a)
        brow.append(b)
        acol.append(a.T)
        bcol.append((-b).T)

    chains = [(e, l) for e in range(2) for l in range(2)]
    for c, (e, l) in enumerate(chains):
        hop = paired(lhop_ref[e, l, 0], lhop_ref[e, l, 1])
        l0 = times_diag(hop.T, arow[e][NB + l:NB + l + 1], brow[e][NB + l:NB + l + 1])
        l0_s[c] = l0
        tf_s[c] = hop
        ts_s[c] = split(hop)
        z0_s[c] = paired(lon_ref[e, l, 0], lon_ref[e, l, 1])
        sig_s[c] = mm(split(l0), double(split(hop)))

    def lead_step(number, _):
        r0, l0, sp = [], [], []
        for c, (e, l) in enumerate(chains):
            z = z0_s[c] + sig_s[c]
            r0.append(split(times_diag(z, arow[e][NB + l:NB + l + 1], brow[e][NB + l:NB + l + 1])))
            l0.append(l0_s[c])
        r1, l1 = [], []
        for c in range(4):
            o = mm(jnp.concatenate([r0[c], split(l0[c])], axis=0), double(r0[c]))
            r1.append(split(o[:W2]))
            l1.append(l0[c] + o[W2:])
        r2, l2 = [], []
        for c in range(4):
            o = mm(jnp.concatenate([r1[c], split(l1[c])], axis=0), double(r1[c]))
            r2.append(split(o[:W2]))
            l2.append(split(l1[c] + o[W2:]))
        w = []
        for c in range(4):
            w.append(split(tf_s[c] + mm(r2[c], double(ts_s[c]))))
        for c, (e, l) in enumerate(chains):
            fresh = mm(l2[c], double(w[c]))
            sig_s[c] = jnp.where(number < reps[e], fresh, sig_s[c])
        return 0

    lax.fori_loop(0, jnp.maximum(reps[0], reps[1]), lead_step, 0)

    for c, (e, l) in enumerate(chains):
        s = sig_s[c]
        lead_ref[e, l, 0] = s[:NORB, :NORB]
        lead_ref[e, l, 1] = s[NORB:, :NORB]

    eye = (lax.broadcasted_iota(jnp.int32, (W2, W2), 0) == lax.broadcasted_iota(jnp.int32, (W2, W2), 1)).astype(F32)
    low_lane = lax.broadcasted_iota(jnp.int32, (W2, W2), 1) < NORB
    sigma = [sig_s[0], sig_s[2]]
    gs, lefts, rights = [], [], []
    for b in range(NB - 1):
        link = paired(coupling_ref[b, 0], coupling_ref[b, 1])
        link_t = link.T
        link_s = double(split(link))
        h = paired(hamil_ref[b, 0], hamil_ref[b, 1])
        r0f, r0, l0 = [], [], []
        for e in range(2):
            ar, br = arow[e][b:b + 1], brow[e][b:b + 1]
            r = times_diag(h + sigma[e], ar, br)
            r0f.append(r)
            r0.append(split(r))
            l0.append(times_diag(link_t, ar, br))
        r1f, r1, l1 = [], [], []
        for e in range(2):
            o = mm(jnp.concatenate([r0[e], split(l0[e])], axis=0), double(r0[e]))
            r1f.append(o[:W2])
            r1.append(split(o[:W2]))
            l1.append(l0[e] + o[W2:])
        r2, l2f, l2, q1f, q1 = [], [], [], [], []
        for e in range(2):
            o = mm(jnp.concatenate([r1[e], split(l1[e]), r0[e]], axis=0), double(r1[e]))
            r2.append(split(o[:W2]))
            l2f.append(l1[e] + o[W2:2 * W2])
            l2.append(split(l2f[e]))
            q1f.append(eye + r0f[e] + r1f[e] + o[2 * W2:])
            q1.append(split(q1f[e]))
        o = mm(jnp.concatenate(r2, axis=0), link_s)
        w = [split(link + o[:W2]), split(link + o[W2:])]
        g_b, left_b, right_b = [], [], []
        for e in range(2):
            o = mm(jnp.concatenate([l2[e], q1[e]], axis=0), double(w[e]))
            sigma[e] = o[:W2]
            ac, bc = acol[e][:, b:b + 1], bcol[e][:, b:b + 1]
            left_b.append(split(diag_times(o[W2:], ac, bc)))
        for e in range(2):
            o = mm(jnp.concatenate([l2[e], q1[e]], axis=0), double(r2[e]))
            ac, bc = acol[e][:, b:b + 1], bcol[e][:, b:b + 1]
            right_b.append(double(split(l2f[e] + o[:W2])))
            g_b.append(diag_times(q1f[e] + o[W2:], ac, bc))
        gs.append(g_b)
        lefts.append(left_b)
        rights.append(right_b)

    b = NB - 1
    h = paired(hamil_ref[b, 0], hamil_ref[b, 1])
    green = []
    for e in range(2):
        r0f = times_diag(h + sigma[e] + sig_s[2 * e + 1], arow[e][b:b + 1], brow[e][b:b + 1])
        r0 = split(r0f)
        r1f = mm(r0, double(r0))
        r1 = split(r1f)
        o = mm(jnp.concatenate([r1, r0], axis=0), double(r1))
        q1 = eye + r0f + r1f + o[W2:]
        qf = q1 + mm(split(q1), double(split(o[:W2])))
        green.append(diag_times(qf, acol[e][:, b:b + 1], bcol[e][:, b:b + 1]))

    def put(b, green):
        other = jnp.concatenate([green[1][NORB:], -green[1][:NORB]], axis=0)
        green_ref[b] = jnp.where(low_lane, green[0], other)

    put(b, green)
    for b in range(NB - 2, -1, -1):
        y = [mm(split(green[e]), rights[b][e]) for e in range(2)]
        green = [gs[b][e] + mm(lefts[b][e], double(split(y[e]))) for e in range(2)]
        put(b, green)


def compute(onsite, hamil, coupling, lead_onsite, lead_hop, counts):
    vmem = pl.BlockSpec(memory_space=pltpu.VMEM)
    return pl.pallas_call(
        compute_kernel,
        name="greens",
        out_shape=(
            jax.ShapeDtypeStruct((NB, W2, W2), F32),
            jax.ShapeDtypeStruct((2, 2, 2, NORB, NORB), F32),
        ),
        in_specs=[pl.BlockSpec(memory_space=pltpu.SMEM)] + [vmem] * 5,
        out_specs=(vmem, vmem),
        scratch_shapes=[
            pltpu.VMEM((4, W2, W2), F32),
            pltpu.VMEM((4, W2, W2), F32),
            pltpu.VMEM((4, W2, 2 * W2), BF16),
            pltpu.VMEM((4, W2, W2), F32),
            pltpu.VMEM((4, W2, W2), F32),
        ],
        compiler_params=pltpu.CompilerParams(vmem_limit_bytes=48 * 1024 * 1024),
    )(counts, onsite[0], hamil[0], coupling[0], lead_onsite[:, 0], lead_hop[:, 0])


def cut_along(array, dim, count):
    before, after = (array.shape[:dim], array.shape[dim + 1 :])
    return jnp.moveaxis(array.reshape(*before, count, -1, *after), dim, 0)


def laid_out(blocks, dim):
    blocks = jnp.moveaxis(blocks, 0, dim)
    lengths = blocks.shape
    return blocks.reshape(*lengths[:dim], lengths[dim] * lengths[dim + 1], *lengths[dim + 2 :])


def joined_exchange(array, axis, axes, splits, concats):
    sizes = [lax.axis_size(a) for a in axes]
    blocks = cut_along(array, splits[0], sizes[0])
    blocks = jnp.moveaxis(cut_along(blocks, splits[1] + 1, sizes[1]), 0, 1)
    inside = blocks.shape[2:]
    blocks = blocks.reshape(-1, *inside)
    blocks = lax.all_to_all(blocks, axis, split_axis=0, concat_axis=0, tiled=True)
    blocks = laid_out(blocks.reshape(*sizes, *inside), concats[0] + 1)
    return laid_out(blocks, concats[1])


def convolve(flattened, kernel, offsets):
    energy_count = flattened.shape[0]
    momenta = flattened.shape[1]
    momentum_axis = jnp.arange(momenta, dtype=jnp.int32)
    difference = (momentum_axis[:, None] - momentum_axis[None, :]) % momenta
    selector = (difference[None, :, :] == momentum_axis[:, None, None]).astype(jnp.float32)
    circulant = jnp.einsum("mq,qkj->mkj", kernel, selector, precision=HIGHEST)
    padded = jnp.pad(flattened, ((energy_count, energy_count), (0, 0), (0, 0)))
    result = jnp.zeros_like(flattened)
    for mode_number in range(NMODE):
        offset_now = offsets[mode_number]
        raised = lax.dynamic_slice_in_dim(padded, energy_count + offset_now, energy_count, 0)
        lowered = lax.dynamic_slice_in_dim(padded, energy_count - offset_now, energy_count, 0)
        result = result + jnp.einsum(
            "kj,ejf->ekf", circulant[mode_number], raised + lowered, precision=HIGHEST
        )
    return result


def shards(onsite, hamil, coupling, lead_onsite, lead_hop, counts, kernel, offsets):
    green, lead_sigma = compute(onsite, hamil, coupling, lead_onsite, lead_hop, counts)
    greens = green.reshape(NB, 2, NORB, 2, NORB).transpose(3, 0, 1, 2, 4)
    per_device = greens.shape[0]
    flattened = greens.reshape(per_device, 1, -1)
    spread = joined_exchange(flattened, ("kpt", "energy"), ("kpt", "energy"), (2, 2), (1, 0))
    mixed = convolve(spread, kernel, offsets)
    gathered = lax.all_to_all(
        lax.all_to_all(mixed, "energy", split_axis=0, concat_axis=2, tiled=True),
        "kpt",
        split_axis=1,
        concat_axis=2,
        tiled=True,
    )
    sigma = gathered.reshape((per_device, 1) + greens.shape[1:])
    return (sigma, lead_sigma[:, None])


def solution(mesh):
    placed = (
        P("kpt", None, None),
        P("kpt", None, None, None, None),
        P("kpt", None, None, None, None),
        P("energy", "kpt", None, None, None, None),
        P("energy", "kpt", None, None, None, None),
        P(),
        P(),
        P(),
    )
    return jax.shard_map(
        shards,
        mesh=mesh,
        in_specs=placed,
        out_specs=(
            P("energy", "kpt", None, None, None, None),
            P("energy", "kpt", None, None, None, None),
        ),
        check_vma=False,
    )
```

```python
import jax
import jax.numpy as jnp
from jax import lax
from jax.experimental import pallas as pl
from jax.experimental.pallas import tpu as pltpu
from jax.sharding import PartitionSpec as P

NORB = 64
W2 = 128
NB = 6
NMODE = 4
BASE_ENERGY = 3.0
BROADENING = 0.1
F32 = jnp.float32
BF16 = jnp.bfloat16
HIGHEST = lax.Precision.HIGHEST


def paired(real, imag):
    upper = jnp.concatenate([real, -imag], axis=1)
    lower = jnp.concatenate([imag, real], axis=1)
    return jnp.concatenate([upper, lower], axis=0)


def split(x):
    high = x.astype(BF16)
    low = (x - high.astype(F32)).astype(BF16)
    return jnp.concatenate([high, low], axis=1)


def tall(x):
    s = split(x)
    return jnp.concatenate([s, s], axis=0)


def mm(left, right):
    o = jnp.dot(left, right, preferred_element_type=F32)
    return o[:, :W2] + o[:, W2:]


def double(s):
    return jnp.concatenate([s, s], axis=0)


def swap_rows(x):
    return jnp.concatenate([x[NORB:], x[:NORB]], axis=0)


def times_diag(x, arow, brow):
    return x * arow + pltpu.roll(x, NORB, 1) * brow


def diag_times(x, acol, bcol):
    return x * acol + swap_rows(x) * bcol


def compute_kernel(counts_ref, onsite_ref, hamil_ref, coupling_ref, lon_ref, lhop_ref, green_ref, lead_ref,
                   l0_s, tf_s, ts_s, z0_s, sig_s):
    pos = lax.axis_index("energy")
    ids = [pos * 2, pos * 2 + 1]
    reps = [counts_ref[i] for i in ids]
    onsite = onsite_ref[...]
    onsite2 = jnp.concatenate([onsite, onsite], axis=1)
    lane = lax.broadcasted_iota(jnp.int32, (8, W2), 1)
    sign = jnp.where(lane < NORB, 1.0, -1.0).astype(F32)
    arow, brow, acol, bcol = [], [], [], []
    for e in range(2):
        energy = BASE_ENERGY + ids[e].astype(F32) * (1.0 / 32.0)
        re = energy - onsite2
        mod = re * re + BROADENING * BROADENING
        a = re / mod
        b = (-BROADENING / mod) * sign
        arow.append(a)
        brow.append(b)
        acol.append(a.T)
        bcol.append((-b).T)

    chains = [(e, l) for e in range(2) for l in range(2)]
    for c, (e, l) in enumerate(chains):
        hop = paired(lhop_ref[e, l, 0], lhop_ref[e, l, 1])
        l0 = times_diag(hop.T, arow[e][NB + l:NB + l + 1], brow[e][NB + l:NB + l + 1])
        l0_s[c] = l0
        tf_s[c] = hop
        ts_s[c] = split(hop)
        z0_s[c] = paired(lon_ref[e, l, 0], lon_ref[e, l, 1])
        sig_s[c] = mm(split(l0), double(split(hop)))

    def lead_step(number, _):
        r0, l0, sp = [], [], []
        for c, (e, l) in enumerate(chains):
            z = z0_s[c] + sig_s[c]
            r0.append(split(times_diag(z, arow[e][NB + l:NB + l + 1], brow[e][NB + l:NB + l + 1])))
            l0.append(l0_s[c])
        r1, l1 = [], []
        for c in range(4):
            o = mm(jnp.concatenate([r0[c], split(l0[c])], axis=0), double(r0[c]))
            r1.append(split(o[:W2]))
            l1.append(l0[c] + o[W2:])
        r2, l2 = [], []
        for c in range(4):
            o = mm(jnp.concatenate([r1[c], split(l1[c])], axis=0), double(r1[c]))
            r2.append(split(o[:W2]))
            l2.append(split(l1[c] + o[W2:]))
        w = []
        for c in range(4):
            w.append(split(tf_s[c] + mm(r2[c], double(ts_s[c]))))
        for c, (e, l) in enumerate(chains):
            fresh = mm(l2[c], double(w[c]))
            sig_s[c] = jnp.where(number < reps[e], fresh, sig_s[c])
        return 0

    lax.fori_loop(0, jnp.maximum(reps[0], reps[1]), lead_step, 0)

    for c, (e, l) in enumerate(chains):
        s = sig_s[c]
        lead_ref[e, l, 0] = s[:NORB, :NORB]
        lead_ref[e, l, 1] = s[NORB:, :NORB]

    eye = (lax.broadcasted_iota(jnp.int32, (W2, W2), 0) == lax.broadcasted_iota(jnp.int32, (W2, W2), 1)).astype(F32)
    low_lane = lax.broadcasted_iota(jnp.int32, (W2, W2), 1) < NORB
    sigma = [sig_s[0], sig_s[2]]
    gs, lefts, rights = [], [], []
    for b in range(NB - 1):
        link = paired(coupling_ref[b, 0], coupling_ref[b, 1])
        link_t = link.T
        link_s = double(split(link))
        h = paired(hamil_ref[b, 0], hamil_ref[b, 1])
        r0f, r0, l0 = [], [], []
        for e in range(2):
            ar, br = arow[e][b:b + 1], brow[e][b:b + 1]
            r = times_diag(h + sigma[e], ar, br)
            r0f.append(r)
            r0.append(split(r))
            l0.append(times_diag(link_t, ar, br))
        r1f, r1, l1 = [], [], []
        for e in range(2):
            o = mm(jnp.concatenate([r0[e], split(l0[e])], axis=0), double(r0[e]))
            r1f.append(o[:W2])
            r1.append(split(o[:W2]))
            l1.append(l0[e] + o[W2:])
        r2, l2f, l2, q1f, q1 = [], [], [], [], []
        for e in range(2):
            o = mm(jnp.concatenate([r1[e], split(l1[e]), r0[e]], axis=0), double(r1[e]))
            r2.append(split(o[:W2]))
            l2f.append(l1[e] + o[W2:2 * W2])
            l2.append(split(l2f[e]))
            q1f.append(eye + r0f[e] + r1f[e] + o[2 * W2:])
            q1.append(split(q1f[e]))
        o = mm(jnp.concatenate(r2, axis=0), link_s)
        w = [split(link + o[:W2]), split(link + o[W2:])]
        g_b, left_b, right_b = [], [], []
        for e in range(2):
            o = mm(jnp.concatenate([l2[e], q1[e]], axis=0), double(w[e]))
            sigma[e] = o[:W2]
            ac, bc = acol[e][:, b:b + 1], bcol[e][:, b:b + 1]
            left_b.append(split(diag_times(o[W2:], ac, bc)))
        for e in range(2):
            o = mm(jnp.concatenate([l2[e], q1[e]], axis=0), double(r2[e]))
            ac, bc = acol[e][:, b:b + 1], bcol[e][:, b:b + 1]
            right_b.append(double(split(l2f[e] + o[:W2])))
            g_b.append(diag_times(q1f[e] + o[W2:], ac, bc))
        gs.append(g_b)
        lefts.append(left_b)
        rights.append(right_b)

    b = NB - 1
    h = paired(hamil_ref[b, 0], hamil_ref[b, 1])
    green = []
    for e in range(2):
        r0f = times_diag(h + sigma[e] + sig_s[2 * e + 1], arow[e][b:b + 1], brow[e][b:b + 1])
        r0 = split(r0f)
        r1f = mm(r0, double(r0))
        r1 = split(r1f)
        o = mm(jnp.concatenate([r1, r0], axis=0), double(r1))
        q1 = eye + r0f + r1f + o[W2:]
        qf = q1 + mm(split(q1), double(split(o[:W2])))
        green.append(diag_times(qf, acol[e][:, b:b + 1], bcol[e][:, b:b + 1]))

    def put(b, green):
        other = jnp.concatenate([green[1][NORB:], -green[1][:NORB]], axis=0)
        green_ref[b] = jnp.where(low_lane, green[0], other)

    put(b, green)
    for b in range(NB - 2, -1, -1):
        y = [mm(split(green[e]), rights[b][e]) for e in range(2)]
        green = [gs[b][e] + mm(lefts[b][e], double(split(y[e]))) for e in range(2)]
        put(b, green)


def compute(onsite, hamil, coupling, lead_onsite, lead_hop, counts):
    vmem = pl.BlockSpec(memory_space=pltpu.VMEM)
    return pl.pallas_call(
        compute_kernel,
        name="greens",
        out_shape=(
            jax.ShapeDtypeStruct((NB, W2, W2), F32),
            jax.ShapeDtypeStruct((2, 2, 2, NORB, NORB), F32),
        ),
        in_specs=[pl.BlockSpec(memory_space=pltpu.SMEM)] + [vmem] * 5,
        out_specs=(vmem, vmem),
        scratch_shapes=[
            pltpu.VMEM((4, W2, W2), F32),
            pltpu.VMEM((4, W2, W2), F32),
            pltpu.VMEM((4, W2, 2 * W2), BF16),
            pltpu.VMEM((4, W2, W2), F32),
            pltpu.VMEM((4, W2, W2), F32),
        ],
        compiler_params=pltpu.CompilerParams(vmem_limit_bytes=48 * 1024 * 1024),
    )(counts, onsite[0], hamil[0], coupling[0], lead_onsite[:, 0], lead_hop[:, 0])


MESH = pl.DeviceIdType.MESH
NK = 48
NZ = 12
NX = 4
NY = 8
TILES = 2 * NK


def ring_step(n):
    half = lax.div(n + 1, 2)
    return jnp.where(lax.rem(n, 2) == 1, 6 - half, 6 + half)


def position():
    pos, k = lax.axis_index("energy"), lax.axis_index("kpt")
    return lax.div(pos, 2), lax.rem(pos, 2), lax.div(k, NX), lax.rem(k, NX)


def greet():
    y, c, z, x = position()
    barrier = pltpu.get_barrier_semaphore()
    me = c * NK + z * NX + x

    def one(i, _):
        t = lax.rem(me + i, TILES)
        pl.semaphore_signal(barrier, inc=1, device_id=(y * 2 + lax.div(t, NK), lax.rem(t, NK)), device_id_type=MESH)
        return 0

    lax.fori_loop(1, TILES, one, 0)
    for step in (1, NY - 1):
        there = lax.rem(y + step, NY)
        pl.semaphore_signal(barrier, inc=1, device_id=(there * 2 + c, z * NX + x), device_id_type=MESH)


def all_greeted():
    pl.semaphore_wait(pltpu.get_barrier_semaphore(), TILES + 1)


def scatter(src, dst, send_sem, recv_sem, grouped):
    y, c, z, x = position()
    me = c * NK + z * NX + x

    def one(i, _):
        n = lax.div(i, 8)
        zz = lax.rem(z + ring_step(n), NZ)
        r = lax.rem(i, 8)
        xx = lax.rem(x + lax.div(r, 2), NX)
        cc = lax.rem(c + lax.rem(r, 2), 2)
        kk = zz * NX + xx
        pltpu.make_async_remote_copy(
            src_ref=src.at[cc * NK + kk],
            dst_ref=dst.at[me],
            send_sem=send_sem,
            recv_sem=recv_sem.at[n] if grouped else recv_sem,
            device_id=(y * 2 + cc, kk),
            device_id_type=MESH,
        ).start()
        return 0

    lax.fori_loop(0, TILES - 8, one, 0)
    lax.fori_loop(TILES - 7, TILES, one, 0)
    pltpu.make_async_copy(src.at[me], dst.at[me], recv_sem.at[NZ - 1] if grouped else recv_sem).start()


def wait_tiles(ref, count, sem):
    part = ref.at[pl.ds(0, count)]
    pltpu.make_async_copy(part, part, sem).wait()


def exchange_body(green_ref, mix_ref, sigma_ref, here, below, above, mixed, send_a, recv_a, send_b, recv_b, send_c, recv_c):
    y, c, z, x = position()
    scatter(green_ref, here, send_a, recv_a, True)

    def forward(n, _):
        wait_tiles(here, 8, recv_a.at[n])
        zs = lax.rem(z - ring_step(n) + NZ, NZ)
        for core in range(2):
            rows = pl.ds(core * NK + zs * NX, NX)
            for step, there, slot in ((1, below, 0), (NY - 1, above, 1)):
                pltpu.make_async_remote_copy(
                    src_ref=here.at[rows],
                    dst_ref=there.at[rows],
                    send_sem=send_b.at[slot],
                    recv_sem=recv_b.at[slot],
                    device_id=(lax.rem(y + step, NY) * 2 + c, z * NX + x),
                    device_id_type=MESH,
                ).start()
        return 0

    lax.fori_loop(0, NZ, forward, 0)
    wait_tiles(below, TILES, recv_b.at[0])
    wait_tiles(above, TILES, recv_b.at[1])

    mix = mix_ref[...]
    mix_high = mix.astype(BF16)
    mix = jnp.concatenate([mix_high, (mix - mix_high.astype(F32)).astype(BF16)], axis=0)
    first = lax.broadcasted_iota(jnp.int32, (NK, W2), 1) < NORB
    low = jnp.where(y > 0, 1.0, 0.0).astype(F32)
    high = jnp.where(y < NY - 1, 1.0, 0.0).astype(F32)
    flat = [r.reshape(TILES * 8, W2) for r in (below, here, above)]
    out = mixed.reshape(TILES * 8, W2)
    for s in range(8):
        t = []
        for r, keep in zip(flat, (low, None, high)):
            for core in range(2):
                v = r[pl.ds(core * NK * 8 + s, NK, stride=8), :]
                t.append(v if keep is None else v * keep)
        w = [pltpu.roll(v, NORB, 1) for v in t]
        for core in range(2):
            q = 2 + core
            x1 = w[q] + jnp.where(first, w[q - 1], w[q + 1])
            x2 = t[q + 1] + t[q - 1]
            x3 = jnp.where(first, w[q + 1] + w[q - 2], w[q + 2] + w[q - 1])
            x4 = t[q + 2] + t[q - 2]
            xs = split(jnp.concatenate([x1, x2, x3, x4], axis=0))
            o = jnp.dot(mix, xs, preferred_element_type=F32)
            o = o[:, :W2] + o[:, W2:]
            out[pl.ds(core * NK * 8 + s, NK, stride=8), :] = o[:NK] + o[NK:]

    scatter(mixed, sigma_ref, send_c, recv_c, False)
    wait_tiles(here, TILES - 1, send_a)
    wait_tiles(below, TILES, send_b.at[0])
    wait_tiles(above, TILES, send_b.at[1])
    wait_tiles(sigma_ref, TILES, recv_c)
    wait_tiles(mixed, TILES - 1, send_c)


def mix_rows(kernel, offsets):
    steps = jnp.arange(1, NMODE + 1, dtype=jnp.int32)
    chosen = jnp.where(offsets[None, :] == steps[:, None], 1.0, 0.0).astype(F32)
    by_step = jnp.sum(chosen[:, :, None] * kernel[None, :, :], axis=1)
    k = jnp.arange(NK, dtype=jnp.int32)
    selector = (((k[:, None] - k[None, :]) % NK)[None] == k[:, None, None]).astype(F32)
    return jnp.einsum("oq,qkj->koj", by_step, selector, precision=HIGHEST).reshape(NK, NMODE * NK)


SCRATCH = [
    pltpu.VMEM((TILES, 8, W2), F32),
    pltpu.VMEM((TILES, 8, W2), F32),
    pltpu.VMEM((TILES, 8, W2), F32),
    pltpu.VMEM((TILES, 8, W2), F32),
    pltpu.SemaphoreType.DMA,
    pltpu.SemaphoreType.DMA((NZ,)),
    pltpu.SemaphoreType.DMA((2,)),
    pltpu.SemaphoreType.DMA((2,)),
    pltpu.SemaphoreType.DMA,
    pltpu.SemaphoreType.DMA,
]


def exchange_kernel(*refs):
    greet()
    all_greeted()
    exchange_body(*refs)


def exchange(green, mix):
    vmem = pl.BlockSpec(memory_space=pltpu.VMEM)
    return pl.pallas_call(
        exchange_kernel,
        name="exchange",
        out_shape=jax.ShapeDtypeStruct((TILES, 8, W2), F32),
        in_specs=[vmem] * 2,
        out_specs=vmem,
        scratch_shapes=SCRATCH,
        compiler_params=pltpu.CompilerParams(collective_id=0, has_side_effects=True),
    )(green, mix)


def shards(onsite, hamil, coupling, lead_onsite, lead_hop, counts, kernel, offsets):
    mix = mix_rows(kernel, offsets)
    green, lead_sigma = compute(onsite, hamil, coupling, lead_onsite, lead_hop, counts)
    sigma = exchange(green.reshape(TILES, 8, W2), mix)
    sigma = sigma.reshape(NB, 2, NORB, 2, NORB).transpose(3, 0, 1, 2, 4)
    return (sigma[:, None], lead_sigma[:, None])


def solution(mesh):
    placed = (
        P("kpt", None, None),
        P("kpt", None, None, None, None),
        P("kpt", None, None, None, None),
        P("energy", "kpt", None, None, None, None),
        P("energy", "kpt", None, None, None, None),
        P(),
        P(),
        P(),
    )
    return jax.shard_map(
        shards,
        mesh=mesh,
        in_specs=placed,
        out_specs=(
            P("energy", "kpt", None, None, None, None),
            P("energy", "kpt", None, None, None, None),
        ),
        check_vma=False,
    )
```

```python
import jax
import jax.numpy as jnp
from jax import lax
from jax.experimental import pallas as pl
from jax.experimental.pallas import tpu as pltpu
from jax.sharding import PartitionSpec as P

NORB = 64
W2 = 128
NB = 6
NMODE = 4
MAXIT = 4
BASE_ENERGY = 3.0
BROADENING = 0.1
F32 = jnp.float32
BF16 = jnp.bfloat16
HIGHEST = lax.Precision.HIGHEST


def paired(real, imag):
    upper = jnp.concatenate([real, -imag], axis=1)
    lower = jnp.concatenate([imag, real], axis=1)
    return jnp.concatenate([upper, lower], axis=0)


def split(x):
    high = x.astype(BF16)
    low = (x - high.astype(F32)).astype(BF16)
    return jnp.concatenate([high, low], axis=1)


def tall(x):
    s = split(x)
    return jnp.concatenate([s, s], axis=0)


def mm(left, right):
    o = jnp.dot(left, right, preferred_element_type=F32)
    return o[:, :W2] + o[:, W2:]


def double(s):
    return jnp.concatenate([s, s], axis=0)


def swap_rows(x):
    return jnp.concatenate([x[NORB:], x[:NORB]], axis=0)


def times_diag(x, arow, brow):
    return x * arow + pltpu.roll(x, NORB, 1) * brow


def diag_times(x, acol, bcol):
    return x * acol + swap_rows(x) * bcol


def compute_body(counts_ref, onsite_ref, hamil_ref, coupling_ref, lon_ref, lhop_ref, green_ref, lead_ref,
                 l0_s, tf_s, ts_s, z0_s, sig_s, loaded):
    pos = lax.axis_index("energy")
    loaded(0)
    ids = [pos * 2, pos * 2 + 1]
    reps = [counts_ref[i] for i in ids]
    onsite = onsite_ref[...]
    onsite2 = jnp.concatenate([onsite, onsite], axis=1)
    lane = lax.broadcasted_iota(jnp.int32, (8, W2), 1)
    sign = jnp.where(lane < NORB, 1.0, -1.0).astype(F32)
    arow, brow, acol, bcol = [], [], [], []
    for e in range(2):
        energy = BASE_ENERGY + ids[e].astype(F32) * (1.0 / 32.0)
        re = energy - onsite2
        mod = re * re + BROADENING * BROADENING
        a = re / mod
        b = (-BROADENING / mod) * sign
        arow.append(a)
        brow.append(b)
        acol.append(a.T)
        bcol.append((-b).T)

    loaded(1)
    chains = [(e, l) for e in range(2) for l in range(2)]
    for c, (e, l) in enumerate(chains):
        hop = paired(lhop_ref[e, l, 0], lhop_ref[e, l, 1])
        l0 = times_diag(hop.T, arow[e][NB + l:NB + l + 1], brow[e][NB + l:NB + l + 1])
        l0_s[c] = l0
        tf_s[c] = hop
        ts_s[c] = split(hop)
        z0_s[c] = paired(lon_ref[e, l, 0], lon_ref[e, l, 1])
        sig_s[c] = mm(split(l0), double(split(hop)))

    def lead_step(number, _):
        r0, l0, sp = [], [], []
        for c, (e, l) in enumerate(chains):
            z = z0_s[c] + sig_s[c]
            r0.append(split(times_diag(z, arow[e][NB + l:NB + l + 1], brow[e][NB + l:NB + l + 1])))
            l0.append(l0_s[c])
        r1, l1 = [], []
        for c in range(4):
            o = mm(jnp.concatenate([r0[c], split(l0[c])], axis=0), double(r0[c]))
            r1.append(split(o[:W2]))
            l1.append(l0[c] + o[W2:])
        r2, l2 = [], []
        for c in range(4):
            o = mm(jnp.concatenate([r1[c], split(l1[c])], axis=0), double(r1[c]))
            r2.append(split(o[:W2]))
            l2.append(split(l1[c] + o[W2:]))
        w = []
        for c in range(4):
            w.append(split(tf_s[c] + mm(r2[c], double(ts_s[c]))))
        for c, (e, l) in enumerate(chains):
            fresh = mm(l2[c], double(w[c]))
            sig_s[c] = jnp.where(number < reps[e], fresh, sig_s[c])
        return 0

    lax.fori_loop(0, MAXIT, lead_step, 0)

    for c, (e, l) in enumerate(chains):
        s = sig_s[c]
        lead_ref[e, l, 0] = s[:NORB, :NORB]
        lead_ref[e, l, 1] = s[NORB:, :NORB]

    loaded(2)
    eye = (lax.broadcasted_iota(jnp.int32, (W2, W2), 0) == lax.broadcasted_iota(jnp.int32, (W2, W2), 1)).astype(F32)
    low_lane = lax.broadcasted_iota(jnp.int32, (W2, W2), 1) < NORB
    sigma = [sig_s[0], sig_s[2]]
    gs, lefts, rights = [], [], []
    for b in range(NB - 1):
        link = paired(coupling_ref[b, 0], coupling_ref[b, 1])
        link_t = link.T
        link_s = double(split(link))
        h = paired(hamil_ref[b, 0], hamil_ref[b, 1])
        r0f, r0, l0 = [], [], []
        for e in range(2):
            ar, br = arow[e][b:b + 1], brow[e][b:b + 1]
            r = times_diag(h + sigma[e], ar, br)
            r0f.append(r)
            r0.append(split(r))
            l0.append(times_diag(link_t, ar, br))
        r1f, r1, l1 = [], [], []
        for e in range(2):
            o = mm(jnp.concatenate([r0[e], split(l0[e])], axis=0), double(r0[e]))
            r1f.append(o[:W2])
            r1.append(split(o[:W2]))
            l1.append(l0[e] + o[W2:])
        r2, l2f, l2, q1f, q1 = [], [], [], [], []
        for e in range(2):
            o = mm(jnp.concatenate([r1[e], split(l1[e]), r0[e]], axis=0), double(r1[e]))
            r2.append(split(o[:W2]))
            l2f.append(l1[e] + o[W2:2 * W2])
            l2.append(split(l2f[e]))
            q1f.append(eye + r0f[e] + r1f[e] + o[2 * W2:])
            q1.append(split(q1f[e]))
        o = mm(jnp.concatenate(r2, axis=0), link_s)
        w = [split(link + o[:W2]), split(link + o[W2:])]
        g_b, left_b, right_b = [], [], []
        for e in range(2):
            o = mm(jnp.concatenate([l2[e], q1[e]], axis=0), double(w[e]))
            sigma[e] = o[:W2]
            ac, bc = acol[e][:, b:b + 1], bcol[e][:, b:b + 1]
            left_b.append(split(diag_times(o[W2:], ac, bc)))
        for e in range(2):
            o = mm(jnp.concatenate([l2[e], q1[e]], axis=0), double(r2[e]))
            ac, bc = acol[e][:, b:b + 1], bcol[e][:, b:b + 1]
            right_b.append(double(split(l2f[e] + o[:W2])))
            g_b.append(diag_times(q1f[e] + o[W2:], ac, bc))
        gs.append(g_b)
        lefts.append(left_b)
        rights.append(right_b)

    b = NB - 1
    h = paired(hamil_ref[b, 0], hamil_ref[b, 1])
    green = []
    for e in range(2):
        r0f = times_diag(h + sigma[e] + sig_s[2 * e + 1], arow[e][b:b + 1], brow[e][b:b + 1])
        r0 = split(r0f)
        r1f = mm(r0, double(r0))
        r1 = split(r1f)
        o = mm(jnp.concatenate([r1, r0], axis=0), double(r1))
        q1 = eye + r0f + r1f + o[W2:]
        qf = q1 + mm(split(q1), double(split(o[:W2])))
        green.append(diag_times(qf, acol[e][:, b:b + 1], bcol[e][:, b:b + 1]))

    def put(b, green):
        other = jnp.concatenate([green[1][NORB:], -green[1][:NORB]], axis=0)
        green_ref[pl.ds(b * 16, 16)] = jnp.where(low_lane, green[0], other).reshape(16, 8, W2)

    put(b, green)
    for b in range(NB - 2, -1, -1):
        y = [mm(split(green[e]), rights[b][e]) for e in range(2)]
        green = [gs[b][e] + mm(lefts[b][e], double(split(y[e]))) for e in range(2)]
        put(b, green)


MESH = pl.DeviceIdType.MESH
NK = 48
NZ = 12
NX = 4
NY = 8
TILES = 2 * NK


def around(i, n):
    return jnp.where(i >= n, i - n, i)


def ring_step(n):
    half = (n + 1) >> 1
    return jnp.where((n & 1) == 1, 6 - half, 6 + half)


class Place:
    def __init__(self):
        pos, k = lax.axis_index("energy"), lax.axis_index("kpt")
        self.y, self.c, self.z, self.x, self.k = pos >> 1, pos & 1, k >> 2, k & 3, k
        self.me = self.c * NK + k
        self.peers = [((self.x + dx) & 3, self.c ^ dc) for dx in range(NX) for dc in range(2)]
        self.up = (around(self.y + 1, NY) * 2 + self.c, k)
        self.down = (around(self.y + NY - 1, NY) * 2 + self.c, k)

    def device(self, zz, r):
        xx, cc = self.peers[r]
        return self.y * 2 + cc, zz * NX + xx

    def tile(self, zz, r):
        xx, cc = self.peers[r]
        return cc * NK + zz * NX + xx


def greet(here):
    barrier = pltpu.get_barrier_semaphore()

    def layer(n, _):
        zz = around(here.z + n, NZ)
        for r in range(8):
            pl.semaphore_signal(barrier, inc=1, device_id=here.device(zz, r), device_id_type=MESH)
        return 0

    for r in range(1, 8):
        pl.semaphore_signal(barrier, inc=1, device_id=here.device(here.z, r), device_id_type=MESH)
    for there in (here.up, here.down):
        pl.semaphore_signal(barrier, inc=1, device_id=there, device_id_type=MESH)
    lax.fori_loop(1, NZ, layer, 0)


def all_greeted():
    pl.semaphore_wait(pltpu.get_barrier_semaphore(), TILES + 1)


def scatter(here, src, dst, send_sem, recv_of):
    def send(n, zz, r):
        pltpu.make_async_remote_copy(
            src_ref=src.at[here.tile(zz, r)],
            dst_ref=dst.at[here.me],
            send_sem=send_sem,
            recv_sem=recv_of(n),
            device_id=here.device(zz, r),
            device_id_type=MESH,
        ).start()

    def layer(n, _):
        zz = around(here.z + ring_step(n), NZ)
        for r in range(8):
            send(n, zz, r)
        return 0

    lax.fori_loop(0, NZ - 1, layer, 0)
    for r in range(1, 8):
        send(NZ - 1, here.z, r)
    pltpu.make_async_copy(src.at[here.me], dst.at[here.me], recv_of(NZ - 1)).start()


def wait_tiles(ref, count, sem):
    part = ref.at[pl.ds(0, count)]
    pltpu.make_async_copy(part, part, sem).wait()


def mix_rows(kernel_ref, offsets_ref):
    q = lax.broadcasted_iota(jnp.int32, (NK, W2), 0)
    i = lax.broadcasted_iota(jnp.int32, (NK, W2), 1)
    total = q + i
    turn = ((total == 0) | (total == NK) | (total == 2 * NK) | (total == 3 * NK)).astype(BF16)
    kernel = kernel_ref[...]
    rows = []
    for o in range(1, NMODE + 1):
        row = jnp.zeros((1, NK), F32)
        for m in range(NMODE):
            row = row + jnp.where(offsets_ref[m] == o, kernel[m:m + 1], 0.0)
        rows.append(row)
    rows = jnp.concatenate(rows + rows, axis=0)
    high = rows.astype(BF16)
    low = (rows - high.astype(F32)).astype(BF16)
    ext = jnp.dot(high, turn, preferred_element_type=F32) + jnp.dot(low, turn, preferred_element_type=F32)
    parts = []
    for o in (0, 2):
        a = jnp.broadcast_to(ext[o:o + 1], (NK, W2))
        b = jnp.broadcast_to(ext[o + 1:o + 2], (NK, W2))
        a = pltpu.roll(a, W2 - NK, 1, stride=1, stride_axis=0)
        b = pltpu.roll(b, 0, 1, stride=1, stride_axis=0)
        parts.append(jnp.where(i < NK, a, jnp.where(i < 2 * NK, b, 0.0)))
    mix = jnp.concatenate(parts, axis=1)
    high = mix.astype(BF16)
    return jnp.concatenate([high, (mix - high.astype(F32)).astype(BF16)], axis=0)


def exchange_body(here, green_ref, mix, own, below, above, mixed, packed, send_a, recv_a, send_b, recv_b, send_c, recv_c):
    scatter(here, green_ref, own, send_a, lambda n: recv_a.at[n])

    def forward(n, _):
        wait_tiles(own, 8, recv_a.at[n])
        zs = around(here.z + NZ - ring_step(n), NZ)
        for core in range(2):
            rows = pl.ds(core * NK + zs * NX, NX)
            for there, land, slot in ((here.up, below, 0), (here.down, above, 1)):
                pltpu.make_async_remote_copy(
                    src_ref=own.at[rows],
                    dst_ref=land.at[rows],
                    send_sem=send_b.at[slot],
                    recv_sem=recv_b.at[slot],
                    device_id=there,
                    device_id_type=MESH,
                ).start()
        return 0

    lax.fori_loop(0, NZ, forward, 0)
    wait_tiles(below, TILES, recv_b.at[0])
    wait_tiles(above, TILES, recv_b.at[1])

    first = lax.broadcasted_iota(jnp.int32, (NK, W2), 1) < NORB
    low = jnp.where(here.y > 0, 1.0, 0.0).astype(F32)
    high = jnp.where(here.y < NY - 1, 1.0, 0.0).astype(F32)
    flat = [r.reshape(TILES * 8, W2) for r in (below, own, above)]
    out = mixed.reshape(TILES * 8, W2)
    gap = jnp.zeros((W2 - 2 * NK, W2), F32)
    for s in range(8):
        t = []
        for r, keep in zip(flat, (low, None, high)):
            for core in range(2):
                v = r[pl.ds(core * NK * 8 + s, NK, stride=8), :]
                t.append(v if keep is None else v * keep)
        w = [pltpu.roll(v, NORB, 1) for v in t]
        for core in range(2):
            q = 2 + core
            x1 = w[q] + jnp.where(first, w[q - 1], w[q + 1])
            x2 = t[q + 1] + t[q - 1]
            x3 = jnp.where(first, w[q + 1] + w[q - 2], w[q + 2] + w[q - 1])
            x4 = t[q + 2] + t[q - 2]
            xs = split(jnp.concatenate([x1, x2, gap, x3, x4, gap], axis=0))
            o = jnp.dot(mix, xs, preferred_element_type=F32)
            o = o[:, :W2] + o[:, W2:]
            out[pl.ds(core * NK * 8 + s, NK, stride=8), :] = o[:NK] + o[NK:]

    scatter(here, mixed, packed, send_c, lambda n: recv_c)
    wait_tiles(own, TILES - 1, send_a)
    wait_tiles(below, TILES, send_b.at[0])
    wait_tiles(above, TILES, send_b.at[1])
    wait_tiles(packed, TILES, recv_c)
    wait_tiles(mixed, TILES - 1, send_c)


def step_kernel(counts_ref, offsets_ref, kernel_ref, onsite_hbm, hamil_hbm, coupling_hbm, lon_hbm, lhop_hbm,
                sigma_ref, lead_ref,
                onsite, hamil, coupling, lon, lhop, green, own, below, above, mixed, packed, l0_s, tf_s, ts_s, z0_s, sig_s,
                load, send_a, recv_a, send_b, recv_b, send_c, recv_c):
    moves = [
        pltpu.make_async_copy(a, b, load.at[i])
        for i, (a, b) in enumerate(
            ((onsite_hbm, onsite), (lhop_hbm, lhop), (lon_hbm, lon), (coupling_hbm, coupling), (hamil_hbm, hamil))
        )
    ]
    for move in moves:
        move.start()
    here = Place()
    greet(here)
    mix = mix_rows(kernel_ref, offsets_ref)

    def loaded(stage):
        for move in (moves[:1], moves[1:3], moves[3:])[stage]:
            move.wait()

    compute_body(counts_ref, onsite, hamil, coupling, lon, lhop, green, lead_ref, l0_s, tf_s, ts_s, z0_s, sig_s, loaded)
    all_greeted()
    exchange_body(here, green, mix, own, below, above, mixed, packed, send_a, recv_a, send_b, recv_b, send_c, recv_c)
    for b in range(NB):
        for part in range(2):
            v = packed[pl.ds(b * 16 + part * 8, 8)].reshape(NORB, W2)
            sigma_ref[0, b, part] = v[:, :NORB]
            sigma_ref[1, b, part] = pltpu.roll(v, NORB, 1)[:, :NORB]


def shards(onsite, hamil, coupling, lead_onsite, lead_hop, counts, kernel, offsets):
    vmem = pl.BlockSpec(memory_space=pltpu.VMEM)
    smem = pl.BlockSpec(memory_space=pltpu.SMEM)
    tiles = pltpu.VMEM((TILES, 8, W2), F32)
    square = pltpu.VMEM((4, W2, W2), F32)
    sigma, lead_sigma = pl.pallas_call(
        step_kernel,
        name="born_step",
        out_shape=(
            jax.ShapeDtypeStruct((2, NB, 2, NORB, NORB), F32),
            jax.ShapeDtypeStruct((2, 2, 2, NORB, NORB), F32),
        ),
        in_specs=[smem, smem, vmem] + [pl.BlockSpec(memory_space=pl.ANY)] * 5,
        out_specs=(vmem, vmem),
        scratch_shapes=[
            pltpu.VMEM((NB + 2, NORB), F32),
            pltpu.VMEM((NB, 2, NORB, NORB), F32),
            pltpu.VMEM((NB - 1, 2, NORB, NORB), F32),
            pltpu.VMEM((2, 2, 2, NORB, NORB), F32),
            pltpu.VMEM((2, 2, 2, NORB, NORB), F32),
            tiles, tiles, tiles, tiles, tiles, tiles,
            square, square, pltpu.VMEM((4, W2, 2 * W2), BF16), square, square,
            pltpu.SemaphoreType.DMA((5,)),
            pltpu.SemaphoreType.DMA,
            pltpu.SemaphoreType.DMA((NZ,)),
            pltpu.SemaphoreType.DMA((2,)),
            pltpu.SemaphoreType.DMA((2,)),
            pltpu.SemaphoreType.DMA,
            pltpu.SemaphoreType.DMA,
        ],
        compiler_params=pltpu.CompilerParams(
            collective_id=0, has_side_effects=True, vmem_limit_bytes=56 * 1024 * 1024
        ),
    )(counts, offsets, kernel, onsite[0], hamil[0], coupling[0], lead_onsite[:, 0], lead_hop[:, 0])
    return (sigma[:, None], lead_sigma[:, None])


def solution(mesh):
    placed = (
        P("kpt", None, None),
        P("kpt", None, None, None, None),
        P("kpt", None, None, None, None),
        P("energy", "kpt", None, None, None, None),
        P("energy", "kpt", None, None, None, None),
        P(),
        P(),
        P(),
    )
    return jax.shard_map(
        shards,
        mesh=mesh,
        in_specs=placed,
        out_specs=(
            P("energy", "kpt", None, None, None, None),
            P("energy", "kpt", None, None, None, None),
        ),
        check_vma=False,
    )
```

```python
import jax
import jax.numpy as jnp
from jax import lax
from jax.experimental import pallas as pl
from jax.experimental.pallas import tpu as pltpu
from jax.sharding import PartitionSpec as P

NORB = 64
W2 = 128
NB = 6
NMODE = 4
MAXIT = 4
BASE_ENERGY = 3.0
BROADENING = 0.1
F32 = jnp.float32
BF16 = jnp.bfloat16
HIGHEST = lax.Precision.HIGHEST


def paired(real, imag):
    upper = jnp.concatenate([real, -imag], axis=1)
    lower = jnp.concatenate([imag, real], axis=1)
    return jnp.concatenate([upper, lower], axis=0)


def split(x):
    high = x.astype(BF16)
    low = (x - high.astype(F32)).astype(BF16)
    return jnp.concatenate([high, low], axis=1)


def tall(x):
    s = split(x)
    return jnp.concatenate([s, s], axis=0)


def mm(left, right):
    o = jnp.dot(left, right, preferred_element_type=F32)
    return o[:, :W2] + o[:, W2:]


def double(s):
    return jnp.concatenate([s, s], axis=0)


def swap_rows(x):
    return jnp.concatenate([x[NORB:], x[:NORB]], axis=0)


def times_diag(x, arow, brow):
    return x * arow + pltpu.roll(x, NORB, 1) * brow


def diag_times(x, acol, bcol):
    return x * acol + swap_rows(x) * bcol


def compute_body(counts_ref, onsite_ref, hamil_ref, coupling_ref, lon_ref, lhop_ref, green_ref, lead_ref,
                 l0_s, tf_s, ts_s, z0_s, sig_s, loaded):
    pos = lax.axis_index("energy")
    loaded(0)
    ids = [pos * 2, pos * 2 + 1]
    reps = [counts_ref[i] for i in ids]
    onsite = onsite_ref[...]
    onsite2 = jnp.concatenate([onsite, onsite], axis=1)
    lane = lax.broadcasted_iota(jnp.int32, (8, W2), 1)
    sign = jnp.where(lane < NORB, 1.0, -1.0).astype(F32)
    arow, brow, acol, bcol = [], [], [], []
    for e in range(2):
        energy = BASE_ENERGY + ids[e].astype(F32) * (1.0 / 32.0)
        re = energy - onsite2
        mod = re * re + BROADENING * BROADENING
        a = re / mod
        b = (-BROADENING / mod) * sign
        arow.append(a)
        brow.append(b)
        acol.append(a.T)
        bcol.append((-b).T)

    loaded(1)
    chains = [(e, l) for e in range(2) for l in range(2)]
    for c, (e, l) in enumerate(chains):
        hop = paired(lhop_ref[e, l, 0], lhop_ref[e, l, 1])
        l0 = times_diag(hop.T, arow[e][NB + l:NB + l + 1], brow[e][NB + l:NB + l + 1])
        l0_s[c] = l0
        tf_s[c] = hop
        ts_s[c] = split(hop)
        z0_s[c] = paired(lon_ref[e, l, 0], lon_ref[e, l, 1])
        sig_s[c] = mm(split(l0), double(split(hop)))

    def lead_step(number, _):
        r0, l0, sp = [], [], []
        for c, (e, l) in enumerate(chains):
            z = z0_s[c] + sig_s[c]
            r0.append(split(times_diag(z, arow[e][NB + l:NB + l + 1], brow[e][NB + l:NB + l + 1])))
            l0.append(l0_s[c])
        r1, l1 = [], []
        for c in range(4):
            o = mm(jnp.concatenate([r0[c], split(l0[c])], axis=0), double(r0[c]))
            r1.append(split(o[:W2]))
            l1.append(l0[c] + o[W2:])
        r2, l2 = [], []
        for c in range(4):
            o = mm(jnp.concatenate([r1[c], split(l1[c])], axis=0), double(r1[c]))
            r2.append(split(o[:W2]))
            l2.append(split(l1[c] + o[W2:]))
        w = []
        for c in range(4):
            w.append(split(tf_s[c] + mm(r2[c], double(ts_s[c]))))
        for c, (e, l) in enumerate(chains):
            fresh = mm(l2[c], double(w[c]))
            sig_s[c] = jnp.where(number < reps[e], fresh, sig_s[c])
        return 0

    lax.fori_loop(0, MAXIT, lead_step, 0)

    for c, (e, l) in enumerate(chains):
        s = sig_s[c]
        lead_ref[e, l, 0] = s[:NORB, :NORB]
        lead_ref[e, l, 1] = s[NORB:, :NORB]

    loaded(2)
    eye = (lax.broadcasted_iota(jnp.int32, (W2, W2), 0) == lax.broadcasted_iota(jnp.int32, (W2, W2), 1)).astype(F32)
    low_lane = lax.broadcasted_iota(jnp.int32, (W2, W2), 1) < NORB
    sigma = [sig_s[0], sig_s[2]]
    gs, lefts, rights = [], [], []
    for b in range(NB - 1):
        link = paired(coupling_ref[b, 0], coupling_ref[b, 1])
        link_t = link.T
        link_s = double(split(link))
        h = paired(hamil_ref[b, 0], hamil_ref[b, 1])
        r0f, r0, l0 = [], [], []
        for e in range(2):
            ar, br = arow[e][b:b + 1], brow[e][b:b + 1]
            r = times_diag(h + sigma[e], ar, br)
            r0f.append(r)
            r0.append(split(r))
            l0.append(times_diag(link_t, ar, br))
        r1f, r1, l1 = [], [], []
        for e in range(2):
            o = mm(jnp.concatenate([r0[e], split(l0[e])], axis=0), double(r0[e]))
            r1f.append(o[:W2])
            r1.append(split(o[:W2]))
            l1.append(l0[e] + o[W2:])
        r2, l2f, l2, q1f, q1 = [], [], [], [], []
        for e in range(2):
            o = mm(jnp.concatenate([r1[e], split(l1[e]), r0[e]], axis=0), double(r1[e]))
            r2.append(split(o[:W2]))
            l2f.append(l1[e] + o[W2:2 * W2])
            l2.append(split(l2f[e]))
            q1f.append(eye + r0f[e] + r1f[e] + o[2 * W2:])
            q1.append(split(q1f[e]))
        o = mm(jnp.concatenate(r2, axis=0), link_s)
        w = [split(link + o[:W2]), split(link + o[W2:])]
        g_b, left_b, right_b = [], [], []
        for e in range(2):
            o = mm(jnp.concatenate([l2[e], q1[e]], axis=0), double(w[e]))
            sigma[e] = o[:W2]
            ac, bc = acol[e][:, b:b + 1], bcol[e][:, b:b + 1]
            left_b.append(split(diag_times(o[W2:], ac, bc)))
        for e in range(2):
            o = mm(jnp.concatenate([l2[e], q1[e]], axis=0), double(r2[e]))
            ac, bc = acol[e][:, b:b + 1], bcol[e][:, b:b + 1]
            right_b.append(double(split(l2f[e] + o[:W2])))
            g_b.append(diag_times(q1f[e] + o[W2:], ac, bc))
        gs.append(g_b)
        lefts.append(left_b)
        rights.append(right_b)

    b = NB - 1
    h = paired(hamil_ref[b, 0], hamil_ref[b, 1])
    green = []
    for e in range(2):
        r0f = times_diag(h + sigma[e] + sig_s[2 * e + 1], arow[e][b:b + 1], brow[e][b:b + 1])
        r0 = split(r0f)
        r1f = mm(r0, double(r0))
        r1 = split(r1f)
        o = mm(jnp.concatenate([r1, r0], axis=0), double(r1))
        q1 = eye + r0f + r1f + o[W2:]
        qf = q1 + mm(split(q1), double(split(o[:W2])))
        green.append(diag_times(qf, acol[e][:, b:b + 1], bcol[e][:, b:b + 1]))

    def put(b, green):
        other = jnp.concatenate([green[1][NORB:], -green[1][:NORB]], axis=0)
        green_ref[pl.ds(b * 16, 16)] = jnp.where(low_lane, green[0], other).reshape(16, 8, W2)

    put(b, green)
    for b in range(NB - 2, -1, -1):
        y = [mm(split(green[e]), rights[b][e]) for e in range(2)]
        green = [gs[b][e] + mm(lefts[b][e], double(split(y[e]))) for e in range(2)]
        put(b, green)


MESH = pl.DeviceIdType.MESH
NK = 48
NZ = 12
NX = 4
NY = 8
TILES = 2 * NK


def around(i, n):
    return jnp.where(i >= n, i - n, i)


def ring_step(n):
    half = (n + 1) >> 1
    return jnp.where((n & 1) == 1, 6 - half, 6 + half)


class Place:
    def __init__(self):
        pos, k = lax.axis_index("energy"), lax.axis_index("kpt")
        self.y, self.c, self.z, self.x, self.k = pos >> 1, pos & 1, k >> 2, k & 3, k
        self.me = self.c * NK + k
        self.peers = [((self.x + dx) & 3, self.c ^ dc) for dx in range(NX) for dc in range(2)]
        self.up = (around(self.y + 1, NY) * 2 + self.c, k)
        self.down = (around(self.y + NY - 1, NY) * 2 + self.c, k)

    def device(self, zz, r):
        xx, cc = self.peers[r]
        return self.y * 2 + cc, zz * NX + xx

    def tile(self, zz, r):
        xx, cc = self.peers[r]
        return cc * NK + zz * NX + xx


def greet(here):
    barrier = pltpu.get_barrier_semaphore()

    def layer(n, _):
        zz = around(here.z + n, NZ)
        for r in range(8):
            pl.semaphore_signal(barrier, inc=1, device_id=here.device(zz, r), device_id_type=MESH)
        return 0

    for r in range(1, 8):
        pl.semaphore_signal(barrier, inc=1, device_id=here.device(here.z, r), device_id_type=MESH)
    for there in (here.up, here.down):
        pl.semaphore_signal(barrier, inc=1, device_id=there, device_id_type=MESH)
    lax.fori_loop(1, NZ, layer, 0)


def all_greeted():
    pl.semaphore_wait(pltpu.get_barrier_semaphore(), TILES + 1)


def scatter(here, half, src, dst, send_sem, recv_of):
    rows = pl.ds(half * 4, 4)

    def send(n, zz, r):
        pltpu.make_async_remote_copy(
            src_ref=src.at[here.tile(zz, r), rows],
            dst_ref=dst.at[here.me, rows],
            send_sem=send_sem,
            recv_sem=recv_of(n),
            device_id=here.device(zz, r),
            device_id_type=MESH,
        ).start()

    def layer(n, _):
        zz = around(here.z + ring_step(n), NZ)
        for r in range(8):
            send(n, zz, r)
        return 0

    lax.fori_loop(0, NZ - 1, layer, 0)
    for r in range(1, 8):
        send(NZ - 1, here.z, r)
    pltpu.make_async_copy(src.at[here.me, rows], dst.at[here.me, rows], recv_of(NZ - 1)).start()


def wait_halves(ref, count, sem):
    part = ref.at[pl.ds(0, count), pl.ds(0, 4)]
    pltpu.make_async_copy(part, part, sem).wait()


def mix_rows(kernel_ref, offsets_ref):
    q = lax.broadcasted_iota(jnp.int32, (NK, W2), 0)
    i = lax.broadcasted_iota(jnp.int32, (NK, W2), 1)
    total = q + i
    turn = ((total == 0) | (total == NK) | (total == 2 * NK) | (total == 3 * NK)).astype(BF16)
    kernel = kernel_ref[...]
    rows = []
    for o in range(1, NMODE + 1):
        row = jnp.zeros((1, NK), F32)
        for m in range(NMODE):
            row = row + jnp.where(offsets_ref[m] == o, kernel[m:m + 1], 0.0)
        rows.append(row)
    rows = jnp.concatenate(rows + rows, axis=0)
    high = rows.astype(BF16)
    low = (rows - high.astype(F32)).astype(BF16)
    ext = jnp.dot(high, turn, preferred_element_type=F32) + jnp.dot(low, turn, preferred_element_type=F32)
    parts = []
    for o in (0, 2):
        a = jnp.broadcast_to(ext[o:o + 1], (NK, W2))
        b = jnp.broadcast_to(ext[o + 1:o + 2], (NK, W2))
        a = pltpu.roll(a, W2 - NK, 1, stride=1, stride_axis=0)
        b = pltpu.roll(b, 0, 1, stride=1, stride_axis=0)
        parts.append(jnp.where(i < NK, a, jnp.where(i < 2 * NK, b, 0.0)))
    mix = jnp.concatenate(parts, axis=1)
    high = mix.astype(BF16)
    return jnp.concatenate([high, (mix - high.astype(F32)).astype(BF16)], axis=0)


def exchange_body(here, green_ref, mix, own, below, above, mixed, packed, send_a, recv_a, send_b, recv_b, send_c, recv_c):
    for half in range(2):
        scatter(here, half, green_ref, own, send_a.at[half], lambda n: recv_a.at[half, n])

    first = lax.broadcasted_iota(jnp.int32, (NK, W2), 1) < NORB
    low = jnp.where(here.y > 0, 1.0, 0.0).astype(F32)
    high = jnp.where(here.y < NY - 1, 1.0, 0.0).astype(F32)
    flat = [r.reshape(TILES * 8, W2) for r in (below, own, above)]
    out = mixed.reshape(TILES * 8, W2)
    gap = jnp.zeros((W2 - 2 * NK, W2), F32)

    for half in range(2):

        def forward(n, _):
            wait_halves(own, 8, recv_a.at[half, n])
            zs = around(here.z + NZ - ring_step(n), NZ)
            for core in range(2):
                part = (pl.ds(core * NK + zs * NX, NX), pl.ds(half * 4, 4))
                for there, land, slot in ((here.up, below, 0), (here.down, above, 1)):
                    pltpu.make_async_remote_copy(
                        src_ref=own.at[part],
                        dst_ref=land.at[part],
                        send_sem=send_b.at[half, slot],
                        recv_sem=recv_b.at[half, slot],
                        device_id=there,
                        device_id_type=MESH,
                    ).start()
            return 0

        lax.fori_loop(0, NZ, forward, 0)
        wait_halves(below, TILES, recv_b.at[half, 0])
        wait_halves(above, TILES, recv_b.at[half, 1])
        for s in range(half * 4, half * 4 + 4):
            t = []
            for r, keep in zip(flat, (low, None, high)):
                for core in range(2):
                    v = r[pl.ds(core * NK * 8 + s, NK, stride=8), :]
                    t.append(v if keep is None else v * keep)
            w = [pltpu.roll(v, NORB, 1) for v in t]
            for core in range(2):
                q = 2 + core
                x1 = w[q] + jnp.where(first, w[q - 1], w[q + 1])
                x2 = t[q + 1] + t[q - 1]
                x3 = jnp.where(first, w[q + 1] + w[q - 2], w[q + 2] + w[q - 1])
                x4 = t[q + 2] + t[q - 2]
                xs = split(jnp.concatenate([x1, x2, gap, x3, x4, gap], axis=0))
                o = jnp.dot(mix, xs, preferred_element_type=F32)
                o = o[:, :W2] + o[:, W2:]
                out[pl.ds(core * NK * 8 + s, NK, stride=8), :] = o[:NK] + o[NK:]
        scatter(here, half, mixed, packed, send_c.at[half], lambda n: recv_c.at[half])

    for half in range(2):
        wait_halves(own, TILES - 1, send_a.at[half])
        wait_halves(below, TILES, send_b.at[half, 0])
        wait_halves(above, TILES, send_b.at[half, 1])
        wait_halves(packed, TILES, recv_c.at[half])
        wait_halves(mixed, TILES - 1, send_c.at[half])


def step_kernel(counts_ref, offsets_ref, kernel_ref, onsite_hbm, hamil_hbm, coupling_hbm, lon_hbm, lhop_hbm,
                sigma_ref, lead_ref,
                onsite, hamil, coupling, lon, lhop, green, own, below, above, mixed, packed, l0_s, tf_s, ts_s, z0_s, sig_s,
                load, send_a, recv_a, send_b, recv_b, send_c, recv_c):
    moves = [
        pltpu.make_async_copy(a, b, load.at[i])
        for i, (a, b) in enumerate(
            ((onsite_hbm, onsite), (lhop_hbm, lhop), (lon_hbm, lon), (coupling_hbm, coupling), (hamil_hbm, hamil))
        )
    ]
    for move in moves:
        move.start()
    here = Place()
    greet(here)
    mix = mix_rows(kernel_ref, offsets_ref)

    def loaded(stage):
        for move in (moves[:1], moves[1:3], moves[3:])[stage]:
            move.wait()

    compute_body(counts_ref, onsite, hamil, coupling, lon, lhop, green, lead_ref, l0_s, tf_s, ts_s, z0_s, sig_s, loaded)
    all_greeted()
    exchange_body(here, green, mix, own, below, above, mixed, packed, send_a, recv_a, send_b, recv_b, send_c, recv_c)
    for b in range(NB):
        for part in range(2):
            v = packed[pl.ds(b * 16 + part * 8, 8)].reshape(NORB, W2)
            sigma_ref[0, b, part] = v[:, :NORB]
            sigma_ref[1, b, part] = pltpu.roll(v, NORB, 1)[:, :NORB]


def shards(onsite, hamil, coupling, lead_onsite, lead_hop, counts, kernel, offsets):
    vmem = pl.BlockSpec(memory_space=pltpu.VMEM)
    smem = pl.BlockSpec(memory_space=pltpu.SMEM)
    tiles = pltpu.VMEM((TILES, 8, W2), F32)
    square = pltpu.VMEM((4, W2, W2), F32)
    sigma, lead_sigma = pl.pallas_call(
        step_kernel,
        name="born_step",
        out_shape=(
            jax.ShapeDtypeStruct((2, NB, 2, NORB, NORB), F32),
            jax.ShapeDtypeStruct((2, 2, 2, NORB, NORB), F32),
        ),
        in_specs=[smem, smem, vmem] + [pl.BlockSpec(memory_space=pl.ANY)] * 5,
        out_specs=(vmem, vmem),
        scratch_shapes=[
            pltpu.VMEM((NB + 2, NORB), F32),
            pltpu.VMEM((NB, 2, NORB, NORB), F32),
            pltpu.VMEM((NB - 1, 2, NORB, NORB), F32),
            pltpu.VMEM((2, 2, 2, NORB, NORB), F32),
            pltpu.VMEM((2, 2, 2, NORB, NORB), F32),
            tiles, tiles, tiles, tiles, tiles, tiles,
            square, square, pltpu.VMEM((4, W2, 2 * W2), BF16), square, square,
            pltpu.SemaphoreType.DMA((5,)),
            pltpu.SemaphoreType.DMA((2,)),
            pltpu.SemaphoreType.DMA((2, NZ)),
            pltpu.SemaphoreType.DMA((2, 2)),
            pltpu.SemaphoreType.DMA((2, 2)),
            pltpu.SemaphoreType.DMA((2,)),
            pltpu.SemaphoreType.DMA((2,)),
        ],
        compiler_params=pltpu.CompilerParams(
            collective_id=0, has_side_effects=True, vmem_limit_bytes=56 * 1024 * 1024
        ),
    )(counts, offsets, kernel, onsite[0], hamil[0], coupling[0], lead_onsite[:, 0], lead_hop[:, 0])
    return (sigma[:, None], lead_sigma[:, None])


def solution(mesh):
    placed = (
        P("kpt", None, None),
        P("kpt", None, None, None, None),
        P("kpt", None, None, None, None),
        P("energy", "kpt", None, None, None, None),
        P("energy", "kpt", None, None, None, None),
        P(),
        P(),
        P(),
    )
    return jax.shard_map(
        shards,
        mesh=mesh,
        in_specs=placed,
        out_specs=(
            P("energy", "kpt", None, None, None, None),
            P("energy", "kpt", None, None, None, None),
        ),
        check_vma=False,
    )
```

```python
import jax
import jax.numpy as jnp
from jax import lax
from jax.experimental import pallas as pl
from jax.experimental.pallas import tpu as pltpu
from jax.sharding import PartitionSpec as P

NORB = 64
W2 = 128
NB = 6
NMODE = 4
MAXIT = 4
BASE_ENERGY = 3.0
BROADENING = 0.1
F32 = jnp.float32
BF16 = jnp.bfloat16
HIGHEST = lax.Precision.HIGHEST


def paired(real, imag):
    upper = jnp.concatenate([real, -imag], axis=1)
    lower = jnp.concatenate([imag, real], axis=1)
    return jnp.concatenate([upper, lower], axis=0)


def split(x):
    high = x.astype(BF16)
    low = (x - high.astype(F32)).astype(BF16)
    return jnp.concatenate([high, low], axis=1)


def tall(x):
    s = split(x)
    return jnp.concatenate([s, s], axis=0)


def mm(left, right):
    o = jnp.dot(left, right, preferred_element_type=F32)
    return o[:, :W2] + o[:, W2:]


def double(s):
    return jnp.concatenate([s, s], axis=0)


def swap_rows(x):
    return jnp.concatenate([x[NORB:], x[:NORB]], axis=0)


def times_diag(x, arow, brow):
    return x * arow + pltpu.roll(x, NORB, 1) * brow


def diag_times(x, acol, bcol):
    return x * acol + swap_rows(x) * bcol


def compute_body(counts_ref, onsite_ref, hamil_ref, coupling_ref, lon_ref, lhop_ref, green_ref, lead_ref,
                 l0_s, tf_s, ts_s, z0_s, sig_s, loaded):
    pos = lax.axis_index("energy")
    loaded(0)
    ids = [pos * 2, pos * 2 + 1]
    reps = [counts_ref[i] for i in ids]
    onsite = onsite_ref[...]
    onsite2 = jnp.concatenate([onsite, onsite], axis=1)
    lane = lax.broadcasted_iota(jnp.int32, (8, W2), 1)
    sign = jnp.where(lane < NORB, 1.0, -1.0).astype(F32)
    arow, brow, acol, bcol = [], [], [], []
    for e in range(2):
        energy = BASE_ENERGY + ids[e].astype(F32) * (1.0 / 32.0)
        re = energy - onsite2
        mod = re * re + BROADENING * BROADENING
        a = re / mod
        b = (-BROADENING / mod) * sign
        arow.append(a)
        brow.append(b)
        acol.append(a.T)
        bcol.append((-b).T)

    loaded(1)
    chains = [(e, l) for e in range(2) for l in range(2)]
    for c, (e, l) in enumerate(chains):
        hop = paired(lhop_ref[e, l, 0], lhop_ref[e, l, 1])
        l0 = times_diag(hop.T, arow[e][NB + l:NB + l + 1], brow[e][NB + l:NB + l + 1])
        l0_s[c] = l0
        tf_s[c] = hop
        ts_s[c] = split(hop)
        z0_s[c] = paired(lon_ref[e, l, 0], lon_ref[e, l, 1])
        sig_s[c] = mm(split(l0), double(split(hop)))

    def lead_step(number, _):
        r0, l0, sp = [], [], []
        for c, (e, l) in enumerate(chains):
            z = z0_s[c] + sig_s[c]
            r0.append(split(times_diag(z, arow[e][NB + l:NB + l + 1], brow[e][NB + l:NB + l + 1])))
            l0.append(l0_s[c])
        r1, l1 = [], []
        for c in range(4):
            o = mm(jnp.concatenate([r0[c], split(l0[c])], axis=0), double(r0[c]))
            r1.append(split(o[:W2]))
            l1.append(l0[c] + o[W2:])
        r2, l2 = [], []
        for c in range(4):
            o = mm(jnp.concatenate([r1[c], split(l1[c])], axis=0), double(r1[c]))
            r2.append(split(o[:W2]))
            l2.append(split(l1[c] + o[W2:]))
        w = []
        for c in range(4):
            w.append(split(tf_s[c] + mm(r2[c], double(ts_s[c]))))
        for c, (e, l) in enumerate(chains):
            fresh = mm(l2[c], double(w[c]))
            sig_s[c] = jnp.where(number < reps[e], fresh, sig_s[c])
        return 0

    lax.fori_loop(0, MAXIT, lead_step, 0)

    for c, (e, l) in enumerate(chains):
        s = sig_s[c]
        lead_ref[e, l, 0] = s[:NORB, :NORB]
        lead_ref[e, l, 1] = s[NORB:, :NORB]

    loaded(2)
    eye = (lax.broadcasted_iota(jnp.int32, (W2, W2), 0) == lax.broadcasted_iota(jnp.int32, (W2, W2), 1)).astype(F32)
    low_lane = lax.broadcasted_iota(jnp.int32, (W2, W2), 1) < NORB
    sigma = [sig_s[0], sig_s[2]]
    gs, lefts, rights = [], [], []
    for b in range(NB - 1):
        link = paired(coupling_ref[b, 0], coupling_ref[b, 1])
        link_t = link.T
        link_s = double(split(link))
        h = paired(hamil_ref[b, 0], hamil_ref[b, 1])
        r0f, r0, l0 = [], [], []
        for e in range(2):
            ar, br = arow[e][b:b + 1], brow[e][b:b + 1]
            r = times_diag(h + sigma[e], ar, br)
            r0f.append(r)
            r0.append(split(r))
            l0.append(times_diag(link_t, ar, br))
        r1f, r1, l1 = [], [], []
        for e in range(2):
            o = mm(jnp.concatenate([r0[e], split(l0[e])], axis=0), double(r0[e]))
            r1f.append(o[:W2])
            r1.append(split(o[:W2]))
            l1.append(l0[e] + o[W2:])
        r2, l2f, l2, q1f, q1 = [], [], [], [], []
        for e in range(2):
            o = mm(jnp.concatenate([r1[e], split(l1[e]), r0[e]], axis=0), double(r1[e]))
            r2.append(split(o[:W2]))
            l2f.append(l1[e] + o[W2:2 * W2])
            l2.append(split(l2f[e]))
            q1f.append(eye + r0f[e] + r1f[e] + o[2 * W2:])
            q1.append(split(q1f[e]))
        o = mm(jnp.concatenate(r2, axis=0), link_s)
        w = [split(link + o[:W2]), split(link + o[W2:])]
        g_b, left_b, right_b = [], [], []
        for e in range(2):
            o = mm(jnp.concatenate([l2[e], q1[e]], axis=0), double(w[e]))
            sigma[e] = o[:W2]
            ac, bc = acol[e][:, b:b + 1], bcol[e][:, b:b + 1]
            left_b.append(split(diag_times(o[W2:], ac, bc)))
        for e in range(2):
            o = mm(jnp.concatenate([l2[e], q1[e]], axis=0), double(r2[e]))
            ac, bc = acol[e][:, b:b + 1], bcol[e][:, b:b + 1]
            right_b.append(double(split(l2f[e] + o[:W2])))
            g_b.append(diag_times(q1f[e] + o[W2:], ac, bc))
        gs.append(g_b)
        lefts.append(left_b)
        rights.append(right_b)

    b = NB - 1
    h = paired(hamil_ref[b, 0], hamil_ref[b, 1])
    green = []
    for e in range(2):
        r0f = times_diag(h + sigma[e] + sig_s[2 * e + 1], arow[e][b:b + 1], brow[e][b:b + 1])
        r0 = split(r0f)
        r1f = mm(r0, double(r0))
        r1 = split(r1f)
        o = mm(jnp.concatenate([r1, r0], axis=0), double(r1))
        q1 = eye + r0f + r1f + o[W2:]
        qf = q1 + mm(split(q1), double(split(o[:W2])))
        green.append(diag_times(qf, acol[e][:, b:b + 1], bcol[e][:, b:b + 1]))

    def put(b, green):
        other = jnp.concatenate([green[1][NORB:], -green[1][:NORB]], axis=0)
        green_ref[pl.ds(b * 16, 16)] = jnp.where(low_lane, green[0], other).reshape(16, 8, W2)

    put(b, green)
    for b in range(NB - 2, -1, -1):
        y = [mm(split(green[e]), rights[b][e]) for e in range(2)]
        green = [gs[b][e] + mm(lefts[b][e], double(split(y[e]))) for e in range(2)]
        put(b, green)


MESH = pl.DeviceIdType.MESH
NK = 48
NZ = 12
NX = 4
NY = 8
TILES = 2 * NK


def around(i, n):
    return jnp.where(i >= n, i - n, i)


def ring_step(n):
    half = (n + 1) >> 1
    return jnp.where((n & 1) == 1, 6 - half, 6 + half)


class Place:
    def __init__(self):
        pos, k = lax.axis_index("energy"), lax.axis_index("kpt")
        self.y, self.c, self.z, self.x, self.k = pos >> 1, pos & 1, k >> 2, k & 3, k
        self.me = self.c * NK + k
        self.peers = [((self.x + dx) & 3, self.c ^ dc) for dx in range(NX) for dc in range(2)]
        self.up = (around(self.y + 1, NY) * 2 + self.c, k)
        self.down = (around(self.y + NY - 1, NY) * 2 + self.c, k)

    def device(self, zz, r):
        xx, cc = self.peers[r]
        return self.y * 2 + cc, zz * NX + xx

    def tile(self, zz, r):
        xx, cc = self.peers[r]
        return cc * NK + zz * NX + xx


def greet(here):
    barrier = pltpu.get_barrier_semaphore()

    def layer(n, _):
        zz = around(here.z + n, NZ)
        for r in range(8):
            pl.semaphore_signal(barrier, inc=1, device_id=here.device(zz, r), device_id_type=MESH)
        return 0

    for r in range(1, 8):
        pl.semaphore_signal(barrier, inc=1, device_id=here.device(here.z, r), device_id_type=MESH)
    for there in (here.up, here.down):
        pl.semaphore_signal(barrier, inc=1, device_id=there, device_id_type=MESH)
    lax.fori_loop(1, NZ, layer, 0)


def all_greeted():
    pl.semaphore_wait(pltpu.get_barrier_semaphore(), TILES + 1)


def scatter(here, half, src, dst, send_sem, recv_of):
    rows = pl.ds(half * 4, 4)

    def send(n, zz, r):
        pltpu.make_async_remote_copy(
            src_ref=src.at[here.tile(zz, r), rows],
            dst_ref=dst.at[here.me, rows],
            send_sem=send_sem,
            recv_sem=recv_of(n),
            device_id=here.device(zz, r),
            device_id_type=MESH,
        ).start()

    def layer(n, _):
        zz = around(here.z + ring_step(n), NZ)
        for r in range(8):
            send(n, zz, r)
        return 0

    lax.fori_loop(0, NZ - 1, layer, 0)
    for r in range(1, 8):
        send(NZ - 1, here.z, r)
    pltpu.make_async_copy(src.at[here.me, rows], dst.at[here.me, rows], recv_of(NZ - 1)).start()


def wait_halves(ref, count, sem):
    part = ref.at[pl.ds(0, count), pl.ds(0, 4)]
    pltpu.make_async_copy(part, part, sem).wait()


def mix_rows(kernel_ref, offsets_ref):
    q = lax.broadcasted_iota(jnp.int32, (NK, W2), 0)
    i = lax.broadcasted_iota(jnp.int32, (NK, W2), 1)
    total = q + i
    turn = ((total == 0) | (total == NK) | (total == 2 * NK) | (total == 3 * NK)).astype(BF16)
    kernel = kernel_ref[...]
    rows = []
    for o in range(1, NMODE + 1):
        row = jnp.zeros((1, NK), F32)
        for m in range(NMODE):
            row = row + jnp.where(offsets_ref[m] == o, kernel[m:m + 1], 0.0)
        rows.append(row)
    rows = jnp.concatenate(rows + rows, axis=0)
    high = rows.astype(BF16)
    low = (rows - high.astype(F32)).astype(BF16)
    ext = jnp.dot(high, turn, preferred_element_type=F32) + jnp.dot(low, turn, preferred_element_type=F32)
    parts = []
    for o in (0, 2):
        a = jnp.broadcast_to(ext[o:o + 1], (NK, W2))
        b = jnp.broadcast_to(ext[o + 1:o + 2], (NK, W2))
        a = pltpu.roll(a, W2 - NK, 1, stride=1, stride_axis=0)
        b = pltpu.roll(b, 0, 1, stride=1, stride_axis=0)
        parts.append(jnp.where(i < NK, a, jnp.where(i < 2 * NK, b, 0.0)))
    mix = jnp.concatenate(parts, axis=1)
    high = mix.astype(BF16)
    return jnp.concatenate([high, (mix - high.astype(F32)).astype(BF16)], axis=0)


def exchange_body(here, green_ref, mix_of, own, below, above, mixed, packed, send_a, recv_a, send_b, recv_b, send_c, recv_c):
    for half in range(2):
        scatter(here, half, green_ref, own, send_a.at[half], lambda n: recv_a.at[half, n])

    mix = mix_of()
    first = lax.broadcasted_iota(jnp.int32, (NK, W2), 1) < NORB
    low = jnp.where(here.y > 0, 1.0, 0.0).astype(F32)
    high = jnp.where(here.y < NY - 1, 1.0, 0.0).astype(F32)
    flat = [r.reshape(TILES * 8, W2) for r in (below, own, above)]
    out = mixed.reshape(TILES * 8, W2)
    gap = jnp.zeros((W2 - 2 * NK, W2), F32)

    for half in range(2):

        def forward(n, _):
            wait_halves(own, 8, recv_a.at[half, n])
            zs = around(here.z + NZ - ring_step(n), NZ)
            for core in range(2):
                part = (pl.ds(core * NK + zs * NX, NX), pl.ds(half * 4, 4))
                for there, land, slot in ((here.up, below, 0), (here.down, above, 1)):
                    pltpu.make_async_remote_copy(
                        src_ref=own.at[part],
                        dst_ref=land.at[part],
                        send_sem=send_b.at[half, slot],
                        recv_sem=recv_b.at[half, slot],
                        device_id=there,
                        device_id_type=MESH,
                    ).start()
            return 0

        lax.fori_loop(0, NZ, forward, 0)
        wait_halves(below, TILES, recv_b.at[half, 0])
        wait_halves(above, TILES, recv_b.at[half, 1])
        for s in range(half * 4, half * 4 + 4):
            t = []
            for r, keep in zip(flat, (low, None, high)):
                for core in range(2):
                    v = r[pl.ds(core * NK * 8 + s, NK, stride=8), :]
                    t.append(v if keep is None else v * keep)
            w = [pltpu.roll(v, NORB, 1) for v in t]
            for core in range(2):
                q = 2 + core
                x1 = w[q] + jnp.where(first, w[q - 1], w[q + 1])
                x2 = t[q + 1] + t[q - 1]
                x3 = jnp.where(first, w[q + 1] + w[q - 2], w[q + 2] + w[q - 1])
                x4 = t[q + 2] + t[q - 2]
                xs = split(jnp.concatenate([x1, x2, gap, x3, x4, gap], axis=0))
                o = jnp.dot(mix, xs, preferred_element_type=F32)
                o = o[:, :W2] + o[:, W2:]
                out[pl.ds(core * NK * 8 + s, NK, stride=8), :] = o[:NK] + o[NK:]
        scatter(here, half, mixed, packed, send_c.at[half], lambda n: recv_c.at[half])

    for half in range(2):
        wait_halves(own, TILES - 1, send_a.at[half])
        wait_halves(below, TILES, send_b.at[half, 0])
        wait_halves(above, TILES, send_b.at[half, 1])
        wait_halves(packed, TILES, recv_c.at[half])
        wait_halves(mixed, TILES - 1, send_c.at[half])


def step_kernel(counts_ref, offsets_ref, kernel_ref, onsite_hbm, hamil_hbm, coupling_hbm, lon_hbm, lhop_hbm,
                packed, lead_ref,
                onsite, hamil, coupling, lon, lhop, green, own, below, above, mixed, l0_s, tf_s, ts_s, z0_s, sig_s,
                load, send_a, recv_a, send_b, recv_b, send_c, recv_c):
    moves = [
        pltpu.make_async_copy(a, b, load.at[i])
        for i, (a, b) in enumerate(
            ((onsite_hbm, onsite), (lhop_hbm, lhop), (lon_hbm, lon), (coupling_hbm, coupling), (hamil_hbm, hamil))
        )
    ]
    for move in moves:
        move.start()
    here = Place()
    greet(here)

    def loaded(stage):
        for move in (moves[:1], moves[1:3], moves[3:])[stage]:
            move.wait()

    compute_body(counts_ref, onsite, hamil, coupling, lon, lhop, green, lead_ref, l0_s, tf_s, ts_s, z0_s, sig_s, loaded)
    all_greeted()
    exchange_body(here, green, lambda: mix_rows(kernel_ref, offsets_ref), own, below, above, mixed, packed, send_a, recv_a, send_b, recv_b, send_c, recv_c)


def unpack_kernel(packed, lead_in, sigma_hbm, lead_hbm, parts, sems):
    moves = [pltpu.make_async_copy(lead_in, lead_hbm, sems.at[NB])]
    moves[0].start()
    for b in range(NB):
        for part in range(2):
            v = packed[pl.ds(b * 16 + part * 8, 8)].reshape(NORB, W2)
            parts[0, b, part] = v[:, :NORB]
            parts[1, b, part] = pltpu.roll(v, NORB, 1)[:, :NORB]
        moves.append(pltpu.make_async_copy(parts.at[:, b], sigma_hbm.at[:, b], sems.at[b]))
        moves[-1].start()
    for move in moves:
        move.wait()


def shards(onsite, hamil, coupling, lead_onsite, lead_hop, counts, kernel, offsets):
    vmem = pl.BlockSpec(memory_space=pltpu.VMEM)
    smem = pl.BlockSpec(memory_space=pltpu.SMEM)
    tiles = pltpu.VMEM((TILES, 8, W2), F32)
    square = pltpu.VMEM((4, W2, W2), F32)
    sigma, lead_sigma = pl.pallas_call(
        step_kernel,
        name="born_step",
        out_shape=(
            jax.ShapeDtypeStruct((TILES, 8, W2), F32),
            jax.ShapeDtypeStruct((2, 2, 2, NORB, NORB), F32),
        ),
        in_specs=[smem, smem, vmem] + [pl.BlockSpec(memory_space=pl.ANY)] * 5,
        out_specs=(vmem, vmem),
        scratch_shapes=[
            pltpu.VMEM((NB + 2, NORB), F32),
            pltpu.VMEM((NB, 2, NORB, NORB), F32),
            pltpu.VMEM((NB - 1, 2, NORB, NORB), F32),
            pltpu.VMEM((2, 2, 2, NORB, NORB), F32),
            pltpu.VMEM((2, 2, 2, NORB, NORB), F32),
            tiles, tiles, tiles, tiles, tiles,
            square, square, pltpu.VMEM((4, W2, 2 * W2), BF16), square, square,
            pltpu.SemaphoreType.DMA((5,)),
            pltpu.SemaphoreType.DMA((2,)),
            pltpu.SemaphoreType.DMA((2, NZ)),
            pltpu.SemaphoreType.DMA((2, 2)),
            pltpu.SemaphoreType.DMA((2, 2)),
            pltpu.SemaphoreType.DMA((2,)),
            pltpu.SemaphoreType.DMA((2,)),
        ],
        compiler_params=pltpu.CompilerParams(
            collective_id=0, has_side_effects=True, vmem_limit_bytes=56 * 1024 * 1024
        ),
    )(counts, offsets, kernel, onsite[0], hamil[0], coupling[0], lead_onsite[:, 0], lead_hop[:, 0])
    anywhere = pl.BlockSpec(memory_space=pl.ANY)
    sigma, lead_sigma = pl.pallas_call(
        unpack_kernel,
        name="unpack",
        out_shape=(
            jax.ShapeDtypeStruct((2, NB, 2, NORB, NORB), F32),
            jax.ShapeDtypeStruct((2, 2, 2, NORB, NORB), F32),
        ),
        in_specs=[vmem, vmem],
        out_specs=(anywhere, anywhere),
        scratch_shapes=[pltpu.VMEM((2, NB, 2, NORB, NORB), F32), pltpu.SemaphoreType.DMA((NB + 1,))],
    )(sigma, lead_sigma)
    return (sigma[:, None], lead_sigma[:, None])


def solution(mesh):
    placed = (
        P("kpt", None, None),
        P("kpt", None, None, None, None),
        P("kpt", None, None, None, None),
        P("energy", "kpt", None, None, None, None),
        P("energy", "kpt", None, None, None, None),
        P(),
        P(),
        P(),
    )
    return jax.shard_map(
        shards,
        mesh=mesh,
        in_specs=placed,
        out_specs=(
            P("energy", "kpt", None, None, None, None),
            P("energy", "kpt", None, None, None, None),
        ),
        check_vma=False,
    )
```
